32 devices in a mesh: layer: 2 (over y), row: 4 (over z), col: 4 (over x, core).
Axes of the slice: x: 2, y: 2, z: 4, core: 2. Of those that a mesh axis runs over, the one named last changes fastest.
Arguments:
- right_side: float32 [16, 4, 64, 128], P(None, 'row', 'layer'), may hold values from -6 to 6
- below: float32 [2, 16, 4, 64, 128], P('layer', None, 'row'), may hold values from -4 to 4
- diag_inverse: float32 [4, 4, 4, 4, 4, 128, 128], P(None, None, 'row', None, 'col'), as said below
- factor_blocks: float32 [4, 4, 4, 128, 128], P('row', 'col'), may hold values from -0.125 to 0.125
- block_row: int32 [4, 4, 4], P('row', 'col'), may hold values from 16 to 63, as said below
- block_col: int32 [4, 4, 4], P('row', 'col'), may hold values from 0 to 47, as said below
Outputs:
- solution: float32 [16, 4, 64, 128], P(None, 'row', 'layer')
The draws below stay inside these ranges and needn't reach their ends.
Inputs may be any that keep to these rules, and one draw needn't show every extreme that they name: block_row[r, c, n] % 4 == r. block_col[r, c, n] % 4 == c, and block_col[r, c, n] // 16 < block_row[r, c, n] // 16. `diag_inverse`: blocks with k < m are zero and blocks with k == m are lower triangular; the diagonal entries of the diagonal blocks lie in 0.5 to 1.5; the other entries below the diagonal are of mean zero with a spread of about 0.5 / sqrt(128) inside the diagonal blocks and 0.5 / sqrt(2048) in the blocks with k > m, not bounded.
All inputs are finite; a program needn't handle non-finite values.
Results may differ from the reference program's by a relative error of at most 0.0001.
Values sent between devices are 32-bit elements; how exact they have to be, the bound alone decides.
A program may use at most 64 MiB of HBM per device.

```python
import jax
import jax.numpy as jnp
from jax import lax

BLK = 128
NB = 16
STEPS = 4
NRHS = 64
NBLK = 4
NBR = 64
ROWS_PER = 16
N_LAYER = 2
N_ROW = 4
N_COL = 4


def block_couples(key):
    shape = (N_ROW, N_COL, NBLK)
    keys = jax.random.split(jax.random.fold_in(key, 7), 4)
    later = jax.random.randint(keys[0], shape, 1, STEPS)
    earlier = jax.random.randint(keys[1], shape, 0, later)
    slot_row = jax.random.randint(keys[2], shape, 0, NB // N_ROW)
    slot_col = jax.random.randint(keys[3], shape, 0, NB // N_COL)
    owner_row = jnp.arange(N_ROW, dtype=jnp.int32)[:, None, None]
    owner_col = jnp.arange(N_COL, dtype=jnp.int32)[None, :, None]
    rows_out = later * NB + slot_row * N_ROW + owner_row
    cols_out = earlier * NB + slot_col * N_COL + owner_col
    return (rows_out.astype(jnp.int32), cols_out.astype(jnp.int32))


def draw_block_row(key, part):
    return block_couples(key)[0]


def draw_block_col(key, part):
    return block_couples(key)[1]


def draw_diag_inverse(key, part):
    shape = (STEPS, NB // N_ROW, N_ROW, NB // N_COL, N_COL, BLK, BLK)
    keys = jax.random.split(jax.random.fold_in(key, 11), 2)
    values = jax.random.normal(keys[0], shape, jnp.float32)
    pivots = jax.random.uniform(keys[1], shape, jnp.float32, 0.5, 1.5)
    block_k = jnp.arange(NB // N_ROW)[None, :, None, None, None, None, None] * N_ROW + jnp.arange(N_ROW)[None, None, :, None, None, None, None]
    block_m = jnp.arange(NB // N_COL)[None, None, None, :, None, None, None] * N_COL + jnp.arange(N_COL)[None, None, None, None, :, None, None]
    inner_i = jnp.arange(BLK)[:, None]
    inner_j = jnp.arange(BLK)[None, :]
    lower_part = values * (0.5 / jnp.sqrt(jnp.float32(NB * BLK))) * (block_k > block_m).astype(jnp.float32)
    diag_part = (values * (0.5 / jnp.sqrt(jnp.float32(BLK))) * (inner_i > inner_j).astype(jnp.float32) + pivots * (inner_i == inner_j).astype(jnp.float32)) * (block_k == block_m).astype(jnp.float32)
    return (lower_part + diag_part).astype(jnp.float32)


def block_scale(key, extent, shards, least, high):
    def one(position, shards_of):
        steps = jax.random.uniform(jax.random.fold_in(jax.random.fold_in(key, 6), position), (shards_of,), jnp.float32, least / len(shards), high / len(shards))
        return jnp.repeat(jnp.exp(steps), extent[position] // shards_of).reshape((-1,) + (1,) * (len(extent) - position - 1))

    loudness = one(*shards[0])
    for cut in shards[1:]:
        loudness = loudness * one(*cut)
    return loudness


def gaussian(rng, dims, spread, most, cuts=(), kind=jnp.bfloat16):
    gain = block_scale(rng, dims, cuts, -0.22, 0.18) if cuts else 1.0
    array = jax.random.normal(rng, dims, jnp.float32) * spread * gain
    return jnp.minimum(jnp.maximum(array, -most), most).astype(kind)


def setup_inputs(seed: int = 0) -> dict:
    streams_of = jax.random.split(jax.random.key(seed), 7)
    return {
        "right_side": gaussian(streams_of[0], (ROWS_PER, N_ROW, NRHS, BLK), 1.0, 6.0, ((1, 4), (2, 2)), jnp.float32),
        "below": gaussian(streams_of[1], (N_LAYER, ROWS_PER, N_ROW, NRHS, BLK), 0.5, 4.0, ((0, 2), (2, 4)), jnp.float32),
        "diag_inverse": draw_diag_inverse(jax.random.fold_in(streams_of[6], 71), 0),
        "factor_blocks": gaussian(streams_of[3], (N_ROW, N_COL, NBLK, BLK, BLK), (BLK * NB) ** -0.5, 0.125, ((0, 4), (1, 4)), jnp.float32),
        "block_row": draw_block_row(jax.random.fold_in(streams_of[6], 71), 0),
        "block_col": draw_block_col(jax.random.fold_in(streams_of[6], 71), 0),
    }


def reference(right_side, below, diag_inverse, factor_blocks, block_row, block_col):
    merged = (right_side - jnp.sum(below, axis=0)).reshape(NBR, NRHS, BLK)
    listed = factor_blocks.reshape(-1, BLK, BLK)
    row_index = block_row.reshape(-1)
    col_index = block_col.reshape(-1)
    inverted_diagonal = diag_inverse.reshape(STEPS, NB, NB, BLK, BLK)
    solution = jnp.zeros((NBR, NRHS, BLK), jnp.float32)
    for current_supernode in range(STEPS):
        chosen = jnp.take(solution, col_index, axis=0)
        products = jnp.einsum("nrb,nab->nra", chosen, listed, precision=lax.Precision.HIGHEST)
        active = (row_index // NB == current_supernode).astype(jnp.float32)
        summed = jax.ops.segment_sum(products * active[:, None, None], row_index, NBR)
        first_row = current_supernode * NB
        target_rows = merged[first_row:first_row + NB] - summed[first_row:first_row + NB]
        solved_values = jnp.einsum("exnc,xvc->evn", inverted_diagonal[current_supernode], target_rows, precision=lax.Precision.HIGHEST)
        solution = solution.at[first_row:first_row + NB].set(solved_values)
    return solution.reshape(ROWS_PER, N_ROW, NRHS, BLK)
```

```python
import functools

import jax
import jax.numpy as jnp
from jax import lax
from jax.experimental import pallas as pl
from jax.experimental.pallas import tpu as pltpu
from jax.sharding import PartitionSpec as P

F32 = jnp.float32
BF16 = jnp.bfloat16
MESH = pl.DeviceIdType.MESH


def halves(value):
    high = value.astype(BF16)
    return high, (value - high.astype(F32)).astype(BF16)


def stacked(value):
    high, low = halves(value)
    return jnp.concatenate([high.astype(F32), low.astype(F32)], axis=0).astype(BF16)


def dot_nt(left, right):
    return lax.dot_general(
        left, right, (((1,), (1,)), ((), ())), preferred_element_type=F32
    )


def kernel(
    dims,
    right_ref,
    below_ref,
    dinv_ref,
    fac_ref,
    row_ref,
    col_ref,
    out_ref,
    right_v,
    dinv_v,
    fac_v,
    dinv_hi,
    dinv_lo,
    fac_hi,
    fac_lo,
    below_first,
    below_rest,
    part,
    recv_part,
    tb,
    xb,
    recv_t,
    prods,
    *rest,
):
    layers, rows, cols, steps, kr, kc, rhs, blk, nblk = dims
    xs = rest[: steps - 1]
    (
        load_sem,
        y_send,
        y_recv,
        a_send,
        a_recv,
        b_send,
        b_recv,
        o_send,
        o_recv,
    ) = rest[steps - 1 :]
    l = lax.axis_index("layer")
    r = lax.axis_index("row")
    c = lax.axis_index("col")

    def reducers(fn, index=None):
        if kr == cols:
            fn()
        else:
            pl.when((c if index is None else index) < kr)(fn)

    def load_dinv(s):
        return pltpu.make_async_copy(dinv_ref.at[s], dinv_v.at[s], load_sem.at[s])

    load_fac = pltpu.make_async_copy(fac_ref, fac_v, load_sem.at[steps])

    def own_rows(layer):
        return pl.ds(pl.multiple_of(layer * rhs, rhs), rhs)

    def load_right():
        return pltpu.make_async_copy(right_ref.at[:, c], right_v, load_sem.at[steps + 1])

    def load_below(first):
        if first:
            return pltpu.make_async_copy(
                below_ref.at[pl.ds(0, 1), c, own_rows(l)], below_first.at[l], y_recv.at[0, l]
            )
        return pltpu.make_async_copy(
            below_ref.at[pl.ds(1, steps - 1), c, own_rows(l)], below_rest.at[l], y_recv.at[1, l]
        )

    def start_loads():
        load_right().start()
        load_below(True).start()
        load_below(False).start()

    reducers(start_loads)
    load_dinv(0).start()
    load_fac.start()
    for s in range(1, steps):
        load_dinv(s).start()

    barrier = pltpu.get_barrier_semaphore()
    for d in range(1, layers):
        pl.semaphore_signal(
            barrier, inc=1, device_id={"layer": lax.rem(l + d, layers)}, device_id_type=MESH
        )
    for d in range(1, cols):
        pl.semaphore_signal(
            barrier, inc=1, device_id={"col": lax.rem(c + d, cols)}, device_id_type=MESH
        )
    for d in range(1, rows):
        pl.semaphore_signal(
            barrier, inc=1, device_id={"row": lax.rem(r + d, rows), "col": r}, device_id_type=MESH
        )
    for d in range(1, cols):
        pl.semaphore_signal(
            barrier, inc=1, device_id={"row": c, "col": lax.rem(c + d, cols)}, device_id_type=MESH
        )

    @pl.when(c != r)
    def _():
        pl.semaphore_signal(barrier, inc=1, device_id={"col": r}, device_id_type=MESH)
        pl.semaphore_signal(barrier, inc=1, device_id={"row": c}, device_id_type=MESH)

    @pl.when(c != r)
    def _():
        pl.semaphore_wait(barrier, layers - 1 + cols - 1 + cols + rows)

    @pl.when(c == r)
    def _():
        pl.semaphore_wait(barrier, layers - 1 + cols - 1 + (cols - 1) + (rows - 1))

    def y_copy(d, first):
        to = lax.rem(l + d, layers)
        k = 0 if first else 1
        if first:
            src = below_ref.at[pl.ds(0, 1), c, own_rows(to)]
            dst = below_first.at[l]
        else:
            src = below_ref.at[pl.ds(1, steps - 1), c, own_rows(to)]
            dst = below_rest.at[l]
        return pltpu.make_async_remote_copy(
            src_ref=src,
            dst_ref=dst,
            send_sem=y_send.at[k, d],
            recv_sem=y_recv.at[k, l],
            device_id={"layer": to},
            device_id_type=MESH,
        )

    def y_wait(first):
        load_below(first).wait()
        for d in range(1, layers):
            frm = lax.rem(l + d, layers)
            k = 0 if first else 1
            dst = (below_first if first else below_rest).at[frm]
            pltpu.make_async_copy(dst, dst, y_recv.at[k, frm]).wait()

    def start_y():
        for first in (True, False):
            for d in range(1, layers):
                y_copy(d, first).start()

    reducers(start_y)

    def a_copy(ra, d):
        to = lax.rem(c + d, cols)
        return pltpu.make_async_remote_copy(
            src_ref=part.at[ra, lax.rem(to, kr)],
            dst_ref=recv_part.at[ra, c],
            send_sem=a_send.at[ra, d],
            recv_sem=a_recv.at[ra, c],
            device_id={"col": to},
            device_id_type=MESH,
        )

    def a_start(ra):
        for d in range(1, cols):
            reducers(lambda d=d: a_copy(ra, d).start(), lax.rem(c + d, cols))

    def a_sum(ra):
        total = part[ra, lax.rem(c, kr)]
        for d in range(1, cols):
            frm = lax.rem(c + d, cols)
            dst = recv_part.at[ra, frm]
            pltpu.make_async_copy(dst, dst, a_recv.at[ra, frm]).wait()
            total = total + recv_part[ra, frm]
        return total

    def b_buf(rb):
        return recv_t.at[rb // 2] if rb % 2 == 0 else xs[rb // 2]

    def b_copy(rb, d):
        return pltpu.make_async_remote_copy(
            src_ref=(tb if rb % 2 == 0 else xb).at[rb // 2],
            dst_ref=b_buf(rb).at[lax.rem(c, kr)],
            send_sem=b_send.at[rb, d],
            recv_sem=b_recv.at[rb, lax.rem(c, kr)],
            device_id={"row": lax.rem(r + d, rows), "col": r},
            device_id_type=MESH,
        )

    def b_start(rb):
        for d in range(rows - 1, 0, -1):
            b_copy(rb, d).start()

        @pl.when(c != r)
        def _():
            b_copy(rb, 0).start()

        @pl.when(c == r)
        def _():
            pltpu.make_async_copy(
                (tb if rb % 2 == 0 else xb).at[rb // 2],
                b_buf(rb).at[lax.rem(c, kr)],
                b_recv.at[rb, lax.rem(c, kr)],
            ).start()

    def b_wait(rb):
        for i in range(kr):
            dst = b_buf(rb).at[i]
            pltpu.make_async_copy(dst, dst, b_recv.at[rb, i]).wait()

    def o_copy(s, d):
        return pltpu.make_async_remote_copy(
            src_ref=xb.at[s],
            dst_ref=out_ref.at[s * kr + lax.rem(c, kr)],
            send_sem=o_send.at[s, d],
            recv_sem=o_recv.at[s, c],
            device_id={"col": lax.rem(c + d, cols)},
            device_id_type=MESH,
        )

    def o_own(s):
        return pltpu.make_async_copy(
            xb.at[s], out_ref.at[s * kr + lax.rem(c, kr)], o_recv.at[s, c]
        )

    def o_start(s):
        for d in range(1, cols):
            o_copy(s, d).start()
        o_own(s).start()

    def o_wait(s, i):
        dst = out_ref.at[s * kr + lax.rem(i, kr)]
        pltpu.make_async_copy(dst, dst, o_recv.at[s, i]).wait()

    def prepare(s):
        load_dinv(s).wait()
        for i in range(kr):
            for m in range(i + 1):
                high, low = halves(dinv_v[s, i, m])
                dinv_hi[s, i * blk : (i + 1) * blk, m * blk : (m + 1) * blk] = high
                dinv_lo[s, i * blk : (i + 1) * blk, m * blk : (m + 1) * blk] = low

    prepare(0)
    load_fac.wait()
    for n in range(nblk):
        high, low = halves(fac_v[n])
        fac_hi[n] = high
        fac_lo[n] = low
        prods[n] = jnp.zeros((rhs, blk), F32)

    def merged(s):
        value = right_v[s]
        for e in range(layers):
            value = value - (below_first[e, 0] if s == 0 else below_rest[e, s - 1])
        return value

    for s in range(steps):
        def target(s=s):
            if s == 0:
                load_right().wait()
                y_wait(True)
                tb[0] = merged(0)
            else:
                if s == 1:
                    y_wait(False)
                tb[s] = merged(s) - a_sum(2 * s - 1)
            b_start(2 * s)

        reducers(target)
        if s == 0:
            for later in range(1, steps):
                prepare(later)
        b_wait(2 * s)
        pieces = [stacked(recv_t[s, m]) for m in range(kc)]
        for i in range(kr):
            left = jnp.concatenate(pieces[: i + 1], axis=1)
            span = (i + 1) * blk
            rows_of = slice(i * blk, (i + 1) * blk)
            both = dot_nt(left, dinv_hi[s, rows_of, :span]) + dot_nt(
                left, dinv_lo[s, rows_of, :span]
            )
            part[2 * s, i] = both[:rhs] + both[rhs:]
        a_start(2 * s)

        def solved(s=s):
            xb[s] = a_sum(2 * s)
            if s + 1 < steps:
                b_start(2 * s + 1)
            o_start(s)

        reducers(solved)
        if s + 1 == steps:
            break
        b_wait(2 * s + 1)
        sums = [jnp.zeros((rhs, blk), F32) for _ in range(kr)]
        for n in range(nblk):
            place = col_ref[n] // cols - s * kc
            chosen = stacked(xs[s][jnp.clip(place, 0, kc - 1)])
            both = dot_nt(chosen, fac_hi[n]) + dot_nt(chosen, fac_lo[n])
            active = jnp.where((place >= 0) & (place < kc), 1.0, 0.0).astype(F32)
            total = prods[n] + (both[:rhs] + both[rhs:]) * active
            prods[n] = total
            goal = row_ref[n] // rows - (s + 1) * kr
            for i in range(kr):
                sums[i] = sums[i] + total * jnp.where(goal == i, 1.0, 0.0).astype(F32)
        for i in range(kr):
            part[2 * s + 1, i] = sums[i]
        a_start(2 * s + 1)

    for s in range(steps):
        reducers(lambda s=s: o_own(s).wait())
        for d in range(1, cols):
            frm = lax.rem(c + d, cols)
            reducers(lambda s=s, frm=frm: o_wait(s, frm), frm)

    def end_sends():
        for first in (True, False):
            for d in range(1, layers):
                y_copy(d, first).wait_send()
        for rb in range(2 * steps - 1):
            for d in range(1, rows):
                b_copy(rb, d).wait_send()

            @pl.when(c != r)
            def _(rb=rb):
                b_copy(rb, 0).wait_send()

        for s in range(steps):
            for d in range(1, cols):
                o_copy(s, d).wait_send()

    reducers(end_sends)
    for ra in range(2 * steps - 1):
        for d in range(1, cols):
            reducers(lambda ra=ra, d=d: a_copy(ra, d).wait_send(), lax.rem(c + d, cols))


def body(sizes, right_side, below, diag_inverse, factor_blocks, block_row, block_col):
    layers, rows, cols = sizes
    steps, kr, _, kc, _, blk, _ = diag_inverse.shape
    rhs = right_side.shape[2]
    nblk = factor_blocks.shape[2]
    assert rows == cols and kr == kc and kr <= cols
    dims = (layers, rows, cols, steps, kr, kc, rhs, blk, nblk)
    any_space = pl.BlockSpec(memory_space=pl.ANY)
    smem = pl.BlockSpec(memory_space=pltpu.SMEM)
    rounds = 2 * steps - 1
    out = pl.pallas_call(
        functools.partial(kernel, dims),
        out_shape=jax.ShapeDtypeStruct((steps * kr, rhs, blk), F32),
        in_specs=[any_space] * 4 + [smem] * 2,
        out_specs=any_space,
        scratch_shapes=[
            pltpu.VMEM((steps, rhs, blk), F32),
            pltpu.VMEM((steps, kr, kc, blk, blk), F32),
            pltpu.VMEM((nblk, blk, blk), F32),
            pltpu.VMEM((steps, kr * blk, kc * blk), BF16),
            pltpu.VMEM((steps, kr * blk, kc * blk), BF16),
            pltpu.VMEM((nblk, blk, blk), BF16),
            pltpu.VMEM((nblk, blk, blk), BF16),
            pltpu.VMEM((layers, 1, rhs, blk), F32),
            pltpu.VMEM((layers, steps - 1, rhs, blk), F32),
            pltpu.VMEM((rounds, kr, rhs, blk), F32),
            pltpu.VMEM((rounds, cols, rhs, blk), F32),
            pltpu.VMEM((steps, rhs, blk), F32),
            pltpu.VMEM((steps, rhs, blk), F32),
            pltpu.VMEM((steps, kc, rhs, blk), F32),
            pltpu.VMEM((nblk, rhs, blk), F32),
        ]
        + [pltpu.VMEM((kc, rhs, blk), F32) for _ in range(steps - 1)]
        + [
            pltpu.SemaphoreType.DMA((steps + 2,)),
            pltpu.SemaphoreType.DMA((2, layers)),
            pltpu.SemaphoreType.DMA((2, layers)),
            pltpu.SemaphoreType.DMA((rounds, cols)),
            pltpu.SemaphoreType.DMA((rounds, cols)),
            pltpu.SemaphoreType.DMA((rounds, rows)),
            pltpu.SemaphoreType.DMA((rounds, kr)),
            pltpu.SemaphoreType.DMA((steps, cols)),
            pltpu.SemaphoreType.DMA((steps, cols)),
        ],
        compiler_params=pltpu.CompilerParams(collective_id=0, has_side_effects=True),
        name="forward_solve",
    )(
        right_side.reshape(steps, kr, rhs, blk),
        below.reshape(steps, kr, -1, blk),
        diag_inverse.reshape(steps, kr, kc, blk, blk),
        factor_blocks.reshape(nblk, blk, blk),
        block_row.reshape(nblk),
        block_col.reshape(nblk),
    )
    return out.reshape(right_side.shape)


def solution(mesh):
    sizes = tuple(mesh.shape[name] for name in ("layer", "row", "col"))
    return jax.shard_map(
        functools.partial(body, sizes),
        mesh=mesh,
        in_specs=(
            P(None, "row", "layer", None),
            P("layer", None, "row", None, None),
            P(None, None, "row", None, "col", None, None),
            P("row", "col", None, None, None),
            P("row", "col", None),
            P("row", "col", None),
        ),
        out_specs=P(None, "row", "layer", None),
        check_vma=False,
    )
```

```python
import functools

import jax
import jax.numpy as jnp
from jax import lax
from jax.experimental import pallas as pl
from jax.experimental.pallas import tpu as pltpu
from jax.sharding import PartitionSpec as P

F32 = jnp.float32
BF16 = jnp.bfloat16
MESH = pl.DeviceIdType.MESH


def halves(value):
    high = value.astype(BF16)
    return high, (value - high.astype(F32)).astype(BF16)


def stacked(value):
    high, low = halves(value)
    return jnp.concatenate([high.astype(F32), low.astype(F32)], axis=0).astype(BF16)


def dot_nn(left, right):
    return lax.dot_general(
        left, right, (((1,), (0,)), ((), ())), preferred_element_type=F32
    )


def kernel(
    dims,
    right_ref,
    below_ref,
    dinv_ref,
    fac_ref,
    row_ref,
    col_ref,
    out_ref,
    right_v,
    dinv_v,
    fac_v,
    dinv_hi,
    dinv_lo,
    fac_hi,
    fac_lo,
    below_first,
    below_rest,
    part,
    recv_part,
    tb,
    recv_t,
    prods,
    terms,
    psum,
    oterms,
    *rest,
):
    layers, rows, cols, steps, kr, kc, rhs, blk, nblk = dims
    xs = rest[: steps - 1]
    (
        load_sem,
        y_send,
        y_recv,
        a_send,
        a_recv,
        b_send,
        b_recv,
        d_send,
        d_recv,
        o_send,
        o_recv,
    ) = rest[steps - 1 :]
    l = lax.axis_index("layer")
    r = lax.axis_index("row")
    c = lax.axis_index("col")

    def reducers(fn, index=None):
        if kr == cols:
            fn()
        else:
            pl.when((c if index is None else index) < kr)(fn)

    def load_dinv(s):
        return pltpu.make_async_copy(dinv_ref.at[s], dinv_v.at[s], load_sem.at[s])

    load_fac = pltpu.make_async_copy(fac_ref, fac_v, load_sem.at[steps])

    def own_rows(layer):
        return pl.ds(pl.multiple_of(layer * rhs, rhs), rhs)

    def load_right():
        return pltpu.make_async_copy(right_ref.at[:, c], right_v, load_sem.at[steps + 1])

    def load_below(first):
        if first:
            return pltpu.make_async_copy(
                below_ref.at[pl.ds(0, 1), c, own_rows(l)], below_first.at[l], y_recv.at[0, l]
            )
        return pltpu.make_async_copy(
            below_ref.at[pl.ds(1, steps - 1), c, own_rows(l)], below_rest.at[l], y_recv.at[1, l]
        )

    def start_loads():
        load_right().start()
        load_below(True).start()
        load_below(False).start()

    reducers(start_loads)
    load_dinv(0).start()
    load_fac.start()
    for s in range(1, steps):
        load_dinv(s).start()

    barrier = pltpu.get_barrier_semaphore()
    for d in range(1, layers):
        pl.semaphore_signal(
            barrier, inc=1, device_id={"layer": lax.rem(l + d, layers)}, device_id_type=MESH
        )
    for d in range(1, cols):
        pl.semaphore_signal(
            barrier, inc=1, device_id={"col": lax.rem(c + d, cols)}, device_id_type=MESH
        )
    for d in range(1, rows):
        pl.semaphore_signal(
            barrier, inc=1, device_id={"row": lax.rem(r + d, rows), "col": r}, device_id_type=MESH
        )
    for d in range(1, cols):
        pl.semaphore_signal(
            barrier, inc=1, device_id={"row": c, "col": lax.rem(c + d, cols)}, device_id_type=MESH
        )

    @pl.when(c != r)
    def _():
        pl.semaphore_signal(barrier, inc=1, device_id={"col": r}, device_id_type=MESH)
        pl.semaphore_signal(barrier, inc=1, device_id={"row": c}, device_id_type=MESH)

    @pl.when(c != r)
    def _():
        pl.semaphore_wait(barrier, layers - 1 + cols - 1 + cols + rows)

    @pl.when(c == r)
    def _():
        pl.semaphore_wait(barrier, layers - 1 + cols - 1 + (cols - 1) + (rows - 1))

    def y_copy(d, first):
        to = lax.rem(l + d, layers)
        k = 0 if first else 1
        if first:
            src = below_ref.at[pl.ds(0, 1), c, own_rows(to)]
            dst = below_first.at[l]
        else:
            src = below_ref.at[pl.ds(1, steps - 1), c, own_rows(to)]
            dst = below_rest.at[l]
        return pltpu.make_async_remote_copy(
            src_ref=src,
            dst_ref=dst,
            send_sem=y_send.at[k, d],
            recv_sem=y_recv.at[k, l],
            device_id={"layer": to},
            device_id_type=MESH,
        )

    def y_wait(first):
        load_below(first).wait()
        for d in range(1, layers):
            frm = lax.rem(l + d, layers)
            k = 0 if first else 1
            dst = (below_first if first else below_rest).at[frm]
            pltpu.make_async_copy(dst, dst, y_recv.at[k, frm]).wait()

    def start_y():
        for first in (True, False):
            for d in range(1, layers):
                y_copy(d, first).start()

    reducers(start_y)

    half = lax.rem(c, 2)
    hk = kr // 2

    def p_copy(ra):
        return pltpu.make_async_remote_copy(
            src_ref=part.at[ra, pl.ds((1 - half) * hk, hk)],
            dst_ref=recv_part.at[ra],
            send_sem=a_send.at[ra],
            recv_sem=a_recv.at[ra],
            device_id={"col": c + 1 - 2 * half},
            device_id_type=MESH,
        )

    def p_sum(ra):
        p_copy(ra).start()
        pltpu.make_async_copy(recv_part.at[ra], recv_part.at[ra], a_recv.at[ra]).wait()
        psum[ra] = part[ra, pl.ds(half * hk, hk)] + recv_part[ra]

    def over_pairs(ref, index):
        blocks = []
        for i in range(kr):
            h, j = i // hk, i % hk
            total = ref[index, h, j]
            for e in range(2, cols, 2):
                total = total + ref[index, e + h, j]
            blocks.append(total)
        return blocks

    def b_copy(d):
        return pltpu.make_async_remote_copy(
            src_ref=tb,
            dst_ref=recv_t.at[lax.rem(c, kr)],
            send_sem=b_send.at[d],
            recv_sem=b_recv.at[lax.rem(c, kr)],
            device_id={"row": lax.rem(r + d, rows), "col": r},
            device_id_type=MESH,
        )

    def b_start():
        for d in range(rows - 1, 0, -1):
            b_copy(d).start()

        @pl.when(c != r)
        def _():
            b_copy(0).start()

        @pl.when(c == r)
        def _():
            pltpu.make_async_copy(
                tb, recv_t.at[lax.rem(c, kr)], b_recv.at[lax.rem(c, kr)]
            ).start()

    def b_wait():
        for i in range(kr):
            dst = recv_t.at[i]
            pltpu.make_async_copy(dst, dst, b_recv.at[i]).wait()

    def d_copy(ra, d):
        return pltpu.make_async_remote_copy(
            src_ref=psum.at[ra],
            dst_ref=terms.at[ra, c],
            send_sem=d_send.at[ra, d],
            recv_sem=d_recv.at[ra, c],
            device_id={"row": lax.rem(r + d, rows), "col": r},
            device_id_type=MESH,
        )

    def d_start(ra):
        for d in range(rows - 1, 0, -1):
            d_copy(ra, d).start()

        @pl.when(c != r)
        def _():
            d_copy(ra, 0).start()

        @pl.when(c == r)
        def _():
            pltpu.make_async_copy(psum.at[ra], terms.at[ra, c], d_recv.at[ra, c]).start()

    def d_sum(ra):
        for e in range(cols):
            dst = terms.at[ra, e]
            pltpu.make_async_copy(dst, dst, d_recv.at[ra, e]).wait()
        return over_pairs(terms, ra)

    def o_copy(s, d):
        return pltpu.make_async_remote_copy(
            src_ref=psum.at[2 * s],
            dst_ref=oterms.at[s, c],
            send_sem=o_send.at[s, d],
            recv_sem=o_recv.at[s, c],
            device_id={"col": lax.rem(c + d, cols)},
            device_id_type=MESH,
        )

    def o_start(s):
        for d in range(1, cols):
            o_copy(s, d).start()
        oterms[s, c] = psum[2 * s]

    def o_finish(s):
        for d in range(1, cols):
            frm = lax.rem(c + d, cols)
            dst = oterms.at[s, frm]
            pltpu.make_async_copy(dst, dst, o_recv.at[s, frm]).wait()
        blocks = over_pairs(oterms, s)
        for i in range(kr):
            out_ref[s * kr + i] = blocks[i]

    def prepare(s):
        load_dinv(s).wait()
        for i in range(kr):
            for m in range(i + 1):
                high, low = halves(dinv_v[s, i, m].T)
                dinv_hi[s, m * blk : (m + 1) * blk, i * blk : (i + 1) * blk] = high
                dinv_lo[s, m * blk : (m + 1) * blk, i * blk : (i + 1) * blk] = low

    prepare(0)
    load_fac.wait()
    for n in range(nblk):
        high, low = halves(fac_v[n].T)
        fac_hi[n] = high
        fac_lo[n] = low
        prods[n] = jnp.zeros((rhs, blk), F32)

    def merged(s):
        value = right_v[s]
        for e in range(layers):
            value = value - (below_first[e, 0] if s == 0 else below_rest[e, s - 1])
        return value

    def first_target():
        load_right().wait()
        y_wait(True)
        tb[...] = merged(0)
        b_start()

    reducers(first_target)
    b_wait()
    goals = [recv_t[m] for m in range(kc)]
    for s in range(steps):
        pieces = [stacked(value) for value in goals]
        for i in range(kr):
            left = jnp.concatenate(pieces[: i + 1], axis=1)
            span = (i + 1) * blk
            rows_of = slice(i * blk, (i + 1) * blk)
            both = dot_nn(left, dinv_hi[s, :span, rows_of]) + dot_nn(
                left, dinv_lo[s, :span, rows_of]
            )
            part[2 * s, i] = both[:rhs] + both[rhs:]
        p_sum(2 * s)
        if s + 1 < steps:
            d_start(2 * s)
        o_start(s)
        if s + 1 < steps:
            prepare(s + 1)
        if s + 1 == steps:
            break
        found = d_sum(2 * s)
        for m in range(kc):
            xs[s][m] = found[m]
        sums = [jnp.zeros((rhs, blk), F32) for _ in range(kr)]
        for n in range(nblk):
            place = col_ref[n] // cols - s * kc
            chosen = stacked(xs[s][jnp.clip(place, 0, kc - 1)])
            both = dot_nn(chosen, fac_hi[n]) + dot_nn(chosen, fac_lo[n])
            active = jnp.where((place >= 0) & (place < kc), 1.0, 0.0).astype(F32)
            total = prods[n] + (both[:rhs] + both[rhs:]) * active
            prods[n] = total
            goal = row_ref[n] // rows - (s + 1) * kr
            for i in range(kr):
                sums[i] = sums[i] - total * jnp.where(goal == i, 1.0, 0.0).astype(F32)
        for i in range(kr):
            part[2 * s + 1, i] = sums[i]

        def add_merged(s=s):
            if s == 0:
                y_wait(False)
            mine = lax.rem(c, kr)
            part[2 * s + 1, mine] = part[2 * s + 1, mine] + merged(s + 1)

        reducers(add_merged)
        p_sum(2 * s + 1)
        d_start(2 * s + 1)
        o_finish(s)
        found = d_sum(2 * s + 1)
        goals = [found[m] for m in range(kc)]

    o_finish(steps - 1)

    def end_sends():
        for first in (True, False):
            for d in range(1, layers):
                y_copy(d, first).wait_send()
        for d in range(1, rows):
            b_copy(d).wait_send()

        @pl.when(c != r)
        def _():
            b_copy(0).wait_send()

    reducers(end_sends)
    for ra in range(2 * steps - 1):
        p_copy(ra).wait_send()
    for s in range(steps):
        for d in range(1, cols):
            o_copy(s, d).wait_send()
    for ra in range(2 * steps - 2):
        for d in range(1, rows):
            d_copy(ra, d).wait_send()

        @pl.when(c != r)
        def _(ra=ra):
            d_copy(ra, 0).wait_send()


def body(sizes, right_side, below, diag_inverse, factor_blocks, block_row, block_col):
    layers, rows, cols = sizes
    steps, kr, _, kc, _, blk, _ = diag_inverse.shape
    rhs = right_side.shape[2]
    nblk = factor_blocks.shape[2]
    assert rows == cols and kr == kc and kr <= cols and kr % 2 == 0 and cols % 2 == 0
    dims = (layers, rows, cols, steps, kr, kc, rhs, blk, nblk)
    any_space = pl.BlockSpec(memory_space=pl.ANY)
    smem = pl.BlockSpec(memory_space=pltpu.SMEM)
    rounds = 2 * steps - 1
    out = pl.pallas_call(
        functools.partial(kernel, dims),
        out_shape=pltpu.VMEM((steps * kr, rhs, blk), F32),
        in_specs=[any_space] * 4 + [smem] * 2,
        out_specs=pl.BlockSpec(memory_space=pltpu.VMEM),
        scratch_shapes=[
            pltpu.VMEM((steps, rhs, blk), F32),
            pltpu.VMEM((steps, kr, kc, blk, blk), F32),
            pltpu.VMEM((nblk, blk, blk), F32),
            pltpu.VMEM((steps, kc * blk, kr * blk), BF16),
            pltpu.VMEM((steps, kc * blk, kr * blk), BF16),
            pltpu.VMEM((nblk, blk, blk), BF16),
            pltpu.VMEM((nblk, blk, blk), BF16),
            pltpu.VMEM((layers, 1, rhs, blk), F32),
            pltpu.VMEM((layers, steps - 1, rhs, blk), F32),
            pltpu.VMEM((rounds, kr, rhs, blk), F32),
            pltpu.VMEM((rounds, kr // 2, rhs, blk), F32),
            pltpu.VMEM((rhs, blk), F32),
            pltpu.VMEM((kc, rhs, blk), F32),
            pltpu.VMEM((nblk, rhs, blk), F32),
            pltpu.VMEM((rounds - 1, cols, kr // 2, rhs, blk), F32),
            pltpu.VMEM((rounds, kr // 2, rhs, blk), F32),
            pltpu.VMEM((steps, cols, kr // 2, rhs, blk), F32),
        ]
        + [pltpu.VMEM((kc, rhs, blk), F32) for _ in range(steps - 1)]
        + [
            pltpu.SemaphoreType.DMA((steps + 2,)),
            pltpu.SemaphoreType.DMA((2, layers)),
            pltpu.SemaphoreType.DMA((2, layers)),
            pltpu.SemaphoreType.DMA((rounds,)),
            pltpu.SemaphoreType.DMA((rounds,)),
            pltpu.SemaphoreType.DMA((rows,)),
            pltpu.SemaphoreType.DMA((kr,)),
            pltpu.SemaphoreType.DMA((rounds - 1, rows)),
            pltpu.SemaphoreType.DMA((rounds - 1, cols)),
            pltpu.SemaphoreType.DMA((steps, cols)),
            pltpu.SemaphoreType.DMA((steps, cols)),
        ],
        compiler_params=pltpu.CompilerParams(collective_id=0, has_side_effects=True),
        name="forward_solve",
    )(
        right_side.reshape(steps, kr, rhs, blk),
        below.reshape(steps, kr, -1, blk),
        diag_inverse.reshape(steps, kr, kc, blk, blk),
        factor_blocks.reshape(nblk, blk, blk),
        block_row.reshape(nblk),
        block_col.reshape(nblk),
    )
    return out.reshape(right_side.shape)


def solution(mesh):
    sizes = tuple(mesh.shape[name] for name in ("layer", "row", "col"))
    return jax.shard_map(
        functools.partial(body, sizes),
        mesh=mesh,
        in_specs=(
            P(None, "row", "layer", None),
            P("layer", None, "row", None, None),
            P(None, None, "row", None, "col", None, None),
            P("row", "col", None, None, None),
            P("row", "col", None),
            P("row", "col", None),
        ),
        out_specs=P(None, "row", "layer", None),
        check_vma=False,
    )
```
